32 devices in a mesh: row: 4 (over y, x), col: 8 (over z, core).
Axes of the slice: x: 2, y: 2, z: 4, core: 2. Of those that a mesh axis runs over, the one named last changes fastest.
Arguments:
- trailing: float32 [3072, 3072], P('row', 'col'), may hold values from -6 to 6, as said below
- v_panels: bfloat16 [3, 3072, 256], P(None, ('row', 'col')), may hold values from -6 to 6
Outputs:
- updated: float32 [3072, 3072], P('row', 'col')
- w_panels: float32 [3, 3072, 256], P(None, ('row', 'col'))
The draws below stay inside these ranges and needn't reach their ends.
Inputs may be any that keep to these rules, and one draw needn't show every extreme that they name: trailing is symmetric: entry (i, j) equals entry (j, i).
All inputs are finite; a program needn't handle non-finite values.
Results may differ from the reference program's by a relative error of at most 0.0003.
Values may be sent and summed in bfloat16 or wider, within the bound.
A program may use at most 64 MiB of HBM per device.

```python
import math
import jax
import jax.numpy as jnp
from jax import lax

K = 256
TICKS = 3
ORDER = 3072


def draw_trailing(key, part):
    base = jax.random.normal(jax.random.fold_in(key, 11), (ORDER, ORDER), jnp.float32)
    mirrored = (base + base.T) * 0.7071067811865476
    return jnp.clip(mirrored, -6.0, 6.0)


def steps_of(rng, dims, pieces, smallest, largest):
    gain = 1.0
    for axis_at, shards_of in pieces:
        draws = jax.random.uniform(jax.random.fold_in(jax.random.fold_in(rng, 6), axis_at), (shards_of,), jnp.float32, smallest / len(pieces), largest / len(pieces))
        gain = gain * jnp.repeat(jnp.exp(draws), dims[axis_at] // shards_of).reshape((-1,) + (1,) * (len(dims) - 1 - axis_at))
    return gain


def scatter_about(stream_key, dims, deviation, reach, cuts=(), held_as=jnp.bfloat16):
    result = deviation * jax.random.normal(stream_key, dims, jnp.float32)
    if cuts:
        result = result * steps_of(stream_key, dims, cuts, -0.22, 0.18)
    return jnp.clip(result, -reach, reach).astype(held_as)


def setup_inputs(seed: int = 0) -> dict:
    splits = jax.random.split(jax.random.key(seed), 3)
    trailing = draw_trailing(jax.random.fold_in(splits[2], 71), 0)
    v_panels = scatter_about(splits[1], (TICKS, ORDER, K), 1.0, 6.0, ((1, 32),))
    return dict(trailing=trailing, v_panels=v_panels)


def reference(trailing, v_panels):
    scaling = 1.0 / math.sqrt(ORDER)
    current = trailing
    w_list = []
    for tick in range(TICKS):
        v_now = v_panels[tick].astype(jnp.float32)
        product = jnp.dot(current, v_now, precision=lax.Precision.HIGHEST, preferred_element_type=jnp.float32)
        w_now = product * scaling
        rows_side = jnp.concatenate([v_now, w_now], axis=1)
        cols_side = jnp.concatenate([w_now, v_now], axis=1)
        update = lax.dot_general(rows_side, cols_side, (((1,), (1,)), ((), ())), precision=lax.Precision.HIGHEST, preferred_element_type=jnp.float32)
        current = current - update * (0.5 * scaling)
        w_list.append(w_now)
    return (current, jnp.stack(w_list, axis=0))
```

```python
import functools
import math

import jax
import jax.numpy as jnp
from jax import lax
from jax.experimental import pallas as pl
from jax.experimental.pallas import tpu as pltpu
from jax.sharding import PartitionSpec as P

MESH = pl.DeviceIdType.MESH
NT = (((1,), (1,)), ((), ()))
NN = (((1,), (0,)), ((), ()))


def dot(a, b, dims):
    return lax.dot_general(a, b, dims, preferred_element_type=jnp.float32)


def kernel(
    nrow, ncol, ratio, scaling,
    a_ref, v_ref, out_ref, w_ref,
    b_ref, vr, vt, part, got, wc, wr,
    v_send, v_recv, vt_send, vt_recv, vx_send, vx_recv,
    rs_send, rs_recv, wc_send, wc_recv, wr_send, wr_recv, local_sem,
):
    ticks, piece, depth = v_ref.shape
    rows_tile, cols_tile = a_ref.shape
    links = ncol // ratio
    r = lax.axis_index("row")
    c = lax.axis_index("col")
    q = c // ratio
    j = c % ratio
    half = 0.5 * scaling

    def rows(at):
        return pl.ds(pl.multiple_of(at * piece, piece), piece)

    def remote(src, dst, send, recv, row, col):
        return pltpu.make_async_remote_copy(
            src_ref=src, dst_ref=dst, send_sem=send, recv_sem=recv,
            device_id=(row, col), device_id_type=MESH,
        )

    from_row, from_col = c // ratio, j * nrow + r
    to_row, to_col = c % nrow, r * ratio + c // nrow
    stays = jnp.logical_and(to_row == r, to_col == c)

    barrier = pltpu.get_barrier_semaphore()
    for i in range(1, nrow):
        pl.semaphore_signal(barrier, inc=1, device_id=((r + i) % nrow, c), device_id_type=MESH)
    for i in range(1, ncol):
        pl.semaphore_signal(barrier, inc=1, device_id=(r, (c + i) % ncol), device_id_type=MESH)

    @pl.when(jnp.logical_not(stays))
    def _():
        pl.semaphore_signal(barrier, inc=1, device_id=(from_row, from_col), device_id_type=MESH)
        pl.semaphore_signal(barrier, inc=1, device_id=(to_row, to_col), device_id_type=MESH)

    pl.semaphore_wait(barrier, nrow + ncol - 2 + jnp.where(stays, 0, 2))

    def v_out(t, i):
        return remote(
            v_ref.at[t], vr.at[t, rows(c)], v_send.at[t, i], v_recv.at[t, c],
            r, ((q + i) % links) * ratio + j,
        )

    def v_side(t, i, k):
        src_col = ((q + i) % links) * ratio + j
        src = v_ref.at[t] if i == 0 else vr.at[t, rows(src_col)]
        return remote(
            src, vr.at[t, rows(src_col)], vx_send.at[t, i, k - 1], v_recv.at[t, src_col],
            r, q * ratio + (j + k) % ratio,
        )

    def v_own(t):
        return pltpu.make_async_copy(v_ref.at[t], vr.at[t, rows(c)], v_recv.at[t, c])

    def v_in(t, col):
        return pltpu.make_async_copy(v_ref.at[t], vr.at[t, rows(col)], v_recv.at[t, col])

    def v_start(t):
        for i in range(1, links):
            v_out(t, i).start()
        for k in range(1, ratio):
            v_side(t, 0, k).start()
        v_own(t).start()

    vt_move = remote(v_ref, vt.at[:, rows(to_row)], vt_send, vt_recv, to_row, to_col)
    vt_in = pltpu.make_async_copy(v_ref, vt.at[:, rows(r)], vt_recv)

    v_start(0)

    @pl.when(stays)
    def _():
        vt_in.start()

    @pl.when(jnp.logical_not(stays))
    def _():
        vt_move.start()

    for t in range(1, ticks):
        v_start(t)

    b_ref[...] = a_ref[...].T

    def v_relay(t):
        for i in range(1, links):
            v_in(t, ((q + i) % links) * ratio + j).wait()
            for k in range(1, ratio):
                v_side(t, i, k).start()

    def v_finish(t):
        v_in(t, c).wait()
        for i in range(links):
            for k in range(1, ratio):
                v_in(t, ((q + i) % links) * ratio + (j + k) % ratio).wait()

    def rs_out(t, i):
        peer = (r + i) % nrow
        return remote(
            part.at[t, rows(peer)], got.at[t, rows(r)], rs_send.at[t, i], rs_recv.at[t, r], peer, c
        )

    def rs_in(t, peer):
        return pltpu.make_async_copy(
            part.at[t, rows(peer)], got.at[t, rows(peer)], rs_recv.at[t, peer]
        )

    def wc_out(t, i):
        peer = (r + i) % nrow
        spot = wc.at[t, :, rows(r)]
        return remote(spot, spot, wc_send.at[t, i], wc_recv.at[t, r], peer, c)

    def wc_in(t, peer):
        spot = wc.at[t, :, rows(peer)]
        return pltpu.make_async_copy(spot, spot, wc_recv.at[t, peer])

    def vt_out(t, i):
        peer = (r + i) % nrow
        spot = vt.at[t, rows(r)]
        return remote(spot, spot, vx_send.at[t, links + i - 1, 0], vx_recv.at[t, r], peer, c)

    def vt_got(t, peer):
        spot = vt.at[t, rows(peer)]
        return pltpu.make_async_copy(spot, spot, vx_recv.at[t, peer])

    source = q == r
    up = jnp.logical_and(q >= r, q < links - 1)
    down = jnp.logical_and(q <= r, q > 0)

    def wr_spot(t, seat, peer):
        return wr.at[t, :, rows(seat * nrow + peer)]

    def wr_out(t, i, way, first):
        peer = (r + i) % nrow
        src = wc.at[t, :, rows(peer)] if first else wr_spot(t, j, peer)
        if way == 0:
            col = c + ratio
        elif way == 1:
            col = c - ratio
        else:
            col = q * ratio + (j + way - 1) % ratio
        return remote(
            src, wr_spot(t, j, peer), wr_send.at[t, i, way], wr_recv.at[t, j * nrow + peer], r, col
        )

    def wr_in(t, seat, peer):
        spot = wr_spot(t, seat, peer)
        return pltpu.make_async_copy(spot, spot, wr_recv.at[t, seat * nrow + peer])

    def wr_keep(t, i):
        peer = (r + i) % nrow
        return pltpu.make_async_copy(
            wc.at[t, :, rows(peer)], wr_spot(t, j, peer), local_sem.at[t, i]
        )

    def wr_ways(t, i, first, act):
        @pl.when(up)
        def _():
            act(wr_out(t, i, 0, first))

        @pl.when(down)
        def _():
            act(wr_out(t, i, 1, first))

        for k in range(1, ratio):
            act(wr_out(t, i, 1 + k, first))

    def start(copy):
        copy.start()

    def wait_send(copy):
        copy.wait_send()

    def update_rows(t):
        out_ref[...] = (out_ref if t else a_ref)[...] - half * (
            dot(vr[t], wc[t, 0], NT) + dot(vr[t], wc[t, 1], NT)
            + dot(wr[t, 0], vt[t], NT) + dot(wr[t, 1], vt[t], NT)
        )

    for t in range(ticks):
        if t == 0:
            v_relay(0)
            v_finish(0)
        high = b_ref[...].astype(jnp.bfloat16)
        low = (b_ref[...] - high.astype(jnp.float32)).astype(jnp.bfloat16)
        part[t] = dot(high, vr[t], NN) + dot(low, vr[t], NN)
        for i in range(1, nrow):
            rs_out(t, i).start()
        if t:
            update_rows(t - 1)
        total = part[t, rows(r)]
        for i in range(1, nrow):
            peer = (r + i) % nrow
            rs_in(t, peer).wait()
            total = total + got[t, rows(peer)]
        total = total * scaling
        head = total.astype(jnp.bfloat16)
        wc[t, 0, rows(r)] = head
        wc[t, 1, rows(r)] = (total - head.astype(jnp.float32)).astype(jnp.bfloat16)
        for i in range(1, nrow):
            wc_out(t, i).start()
        if t == 0:
            @pl.when(stays)
            def _():
                vt_in.wait()

            @pl.when(jnp.logical_not(stays))
            def _():
                vt_move.wait()

        for i in range(1, nrow):
            vt_out(t, i).start()

        @pl.when(source)
        def _():
            for i in range(nrow):
                if i:
                    wc_in(t, (r + i) % nrow).wait()
                wr_ways(t, i, True, start)
                wr_keep(t, i).start()

        @pl.when(jnp.logical_not(source))
        def _():
            for i in range(nrow):
                wr_in(t, j, (r + i) % nrow).wait()
                wr_ways(t, i, False, start)
            for i in range(1, nrow):
                wc_in(t, (r + i) % nrow).wait()

        if t < ticks - 1:
            v_relay(t + 1)
            b_ref[...] -= half * (dot(wc[t, 0], vr[t], NT) + dot(wc[t, 1], vr[t], NT))
            v_finish(t + 1)

        for i in range(1, nrow):
            vt_got(t, (r + i) % nrow).wait()

        @pl.when(source)
        def _():
            for i in range(nrow):
                wr_keep(t, i).wait()

        for k in range(1, ratio):
            for i in range(nrow):
                wr_in(t, (j + k) % ratio, (r + i) % nrow).wait()
        if t < ticks - 1:
            b_ref[...] -= half * (dot(vt[t], wr[t, 0], NT) + dot(vt[t], wr[t, 1], NT))
        mine = rows(c)
        w_ref[t] = wr[t, 0, mine].astype(jnp.float32) + wr[t, 1, mine].astype(jnp.float32)
    update_rows(ticks - 1)

    for t in range(ticks):
        for i in range(1, links):
            v_out(t, i).wait_send()
        for i in range(links):
            for k in range(1, ratio):
                v_side(t, i, k).wait_send()
        for i in range(1, nrow):
            rs_out(t, i).wait_send()
            wc_out(t, i).wait_send()
            vt_out(t, i).wait_send()

        @pl.when(source)
        def _():
            for i in range(nrow):
                wr_ways(t, i, True, wait_send)

        @pl.when(jnp.logical_not(source))
        def _():
            for i in range(nrow):
                wr_ways(t, i, False, wait_send)


def on_device(trailing, v_panels):
    nrow = lax.axis_size("row")
    ncol = lax.axis_size("col")
    rows_tile, cols_tile = trailing.shape
    ticks, piece, depth = v_panels.shape
    ratio = rows_tile // cols_tile
    links = ncol // ratio
    scaling = 1.0 / math.sqrt(rows_tile * nrow)
    dma = pltpu.SemaphoreType.DMA
    vmem = pl.BlockSpec(memory_space=pltpu.VMEM)
    return pl.pallas_call(
        functools.partial(kernel, nrow, ncol, ratio, scaling),
        out_shape=(
            jax.ShapeDtypeStruct(trailing.shape, jnp.float32),
            jax.ShapeDtypeStruct(v_panels.shape, jnp.float32),
        ),
        in_specs=[vmem, vmem],
        out_specs=(vmem, vmem),
        scratch_shapes=[
            pltpu.VMEM((cols_tile, rows_tile), jnp.float32),
            pltpu.VMEM((ticks, rows_tile, depth), jnp.bfloat16),
            pltpu.VMEM((ticks, cols_tile, depth), jnp.bfloat16),
            pltpu.VMEM((ticks, cols_tile, depth), jnp.float32),
            pltpu.VMEM((ticks, cols_tile, depth), jnp.float32),
            pltpu.VMEM((ticks, 2, cols_tile, depth), jnp.bfloat16),
            pltpu.VMEM((ticks, 2, rows_tile, depth), jnp.bfloat16),
            dma((ticks, links)),
            dma((ticks, ncol)),
            dma,
            dma,
            dma((ticks, links + nrow, ratio)),
            dma((ticks, nrow)),
            dma((ticks, nrow)),
            dma((ticks, nrow)),
            dma((ticks, nrow)),
            dma((ticks, nrow)),
            dma((ticks, nrow, ratio + 1)),
            dma((ticks, ncol)),
            dma((ticks, nrow)),
        ],
        compiler_params=pltpu.CompilerParams(collective_id=0, has_side_effects=True),
    )(trailing, v_panels)


def solution(mesh):
    in_specs = (P("row", "col"), P(None, ("row", "col"), None))
    out_specs = (P("row", "col"), P(None, ("row", "col"), None))
    return jax.shard_map(
        on_device, mesh=mesh, in_specs=in_specs, out_specs=out_specs, check_vma=False
    )
```

```python
import functools
import math

import jax
import jax.numpy as jnp
from jax import lax
from jax.experimental import pallas as pl
from jax.experimental.pallas import tpu as pltpu
from jax.sharding import PartitionSpec as P

MESH = pl.DeviceIdType.MESH
SPLITS = 3
NT = (((1,), (1,)), ((), ()))
NN = (((1,), (0,)), ((), ()))


def dot(a, b, dims):
    return lax.dot_general(a, b, dims, preferred_element_type=jnp.float32)


def kernel(
    nrow, ncol, ratio, scaling,
    a_ref, v_ref, out_ref, w_ref,
    b_ref, vr, vt, part, got, wc, wr,
    v_send, v_recv, vt_send, vt_recv, vx_send, vx_recv,
    rs_send, rs_recv, wc_send, wc_recv, wr_send, wr_recv, local_sem,
):
    ticks, piece, depth = v_ref.shape
    rows_tile, cols_tile = a_ref.shape
    links = ncol // ratio
    r = lax.axis_index("row")
    c = lax.axis_index("col")
    q = c // ratio
    j = c % ratio
    half = 0.5 * scaling

    splits = rs_recv.shape[1]
    chunk = piece // splits

    def rows(at):
        return pl.ds(pl.multiple_of(at * piece, piece), piece)

    def some(at, s):
        return pl.ds(pl.multiple_of(at * piece + s * chunk, chunk), chunk)

    def remote(src, dst, send, recv, row, col):
        return pltpu.make_async_remote_copy(
            src_ref=src, dst_ref=dst, send_sem=send, recv_sem=recv,
            device_id=(row, col), device_id_type=MESH,
        )

    from_row, from_col = c // ratio, j * nrow + r
    to_row, to_col = c % nrow, r * ratio + c // nrow
    stays = jnp.logical_and(to_row == r, to_col == c)

    barrier = pltpu.get_barrier_semaphore()
    for i in range(1, nrow):
        pl.semaphore_signal(barrier, inc=1, device_id=((r + i) % nrow, c), device_id_type=MESH)
    for i in range(1, ncol):
        pl.semaphore_signal(barrier, inc=1, device_id=(r, (c + i) % ncol), device_id_type=MESH)

    @pl.when(jnp.logical_not(stays))
    def _():
        pl.semaphore_signal(barrier, inc=1, device_id=(from_row, from_col), device_id_type=MESH)
        pl.semaphore_signal(barrier, inc=1, device_id=(to_row, to_col), device_id_type=MESH)

    pl.semaphore_wait(barrier, nrow + ncol - 2 + jnp.where(stays, 0, 2))

    def v_out(t, i):
        return remote(
            v_ref.at[t], vr.at[t, rows(c)], v_send.at[t, i], v_recv.at[t, c],
            r, ((q + i) % links) * ratio + j,
        )

    def v_side(t, i, k):
        src_col = ((q + i) % links) * ratio + j
        src = v_ref.at[t] if i == 0 else vr.at[t, rows(src_col)]
        return remote(
            src, vr.at[t, rows(src_col)], vx_send.at[t, i, k - 1], v_recv.at[t, src_col],
            r, q * ratio + (j + k) % ratio,
        )

    def v_own(t):
        return pltpu.make_async_copy(v_ref.at[t], vr.at[t, rows(c)], v_recv.at[t, c])

    def v_in(t, col):
        return pltpu.make_async_copy(v_ref.at[t], vr.at[t, rows(col)], v_recv.at[t, col])

    def v_start(t):
        for i in range(1, links):
            v_out(t, i).start()
        for k in range(1, ratio):
            v_side(t, 0, k).start()
        v_own(t).start()

    vt_move = remote(v_ref, vt.at[:, rows(to_row)], vt_send, vt_recv, to_row, to_col)
    vt_in = pltpu.make_async_copy(v_ref, vt.at[:, rows(r)], vt_recv)

    v_start(0)

    @pl.when(stays)
    def _():
        vt_in.start()

    @pl.when(jnp.logical_not(stays))
    def _():
        vt_move.start()

    for t in range(1, ticks):
        v_start(t)

    b_ref[...] = a_ref[...].T

    def v_relay(t):
        for i in range(1, links):
            v_in(t, ((q + i) % links) * ratio + j).wait()
            for k in range(1, ratio):
                v_side(t, i, k).start()

    def v_finish(t):
        v_in(t, c).wait()
        for i in range(links):
            for k in range(1, ratio):
                v_in(t, ((q + i) % links) * ratio + (j + k) % ratio).wait()

    def rs_out(t, s, i):
        peer = (r + i) % nrow
        return remote(
            part.at[t, some(peer, s)], got.at[t, some(r, s)],
            rs_send.at[t, s, i], rs_recv.at[t, s, r], peer, c,
        )

    def rs_in(t, s, peer):
        return pltpu.make_async_copy(
            part.at[t, some(peer, s)], got.at[t, some(peer, s)], rs_recv.at[t, s, peer]
        )

    def wc_out(t, s, i):
        peer = (r + i) % nrow
        spot = wc.at[t, :, some(r, s)]
        return remote(spot, spot, wc_send.at[t, s, i], wc_recv.at[t, s, r], peer, c)

    def wc_in(t, s, peer):
        spot = wc.at[t, :, some(peer, s)]
        return pltpu.make_async_copy(spot, spot, wc_recv.at[t, s, peer])

    def vt_out(t, i):
        peer = (r + i) % nrow
        spot = vt.at[t, rows(r)]
        return remote(spot, spot, vx_send.at[t, links + i - 1, 0], vx_recv.at[t, r], peer, c)

    def vt_got(t, peer):
        spot = vt.at[t, rows(peer)]
        return pltpu.make_async_copy(spot, spot, vx_recv.at[t, peer])

    source = q == r
    up = jnp.logical_and(q >= r, q < links - 1)
    down = jnp.logical_and(q <= r, q > 0)

    def wr_spot(t, s, seat, peer):
        return wr.at[t, :, some(seat * nrow + peer, s)]

    def wr_out(t, s, i, way, first):
        peer = (r + i) % nrow
        spot = wr_spot(t, s, j, peer)
        src = wc.at[t, :, some(peer, s)] if first else spot
        if way == 0:
            col = c + ratio
        elif way == 1:
            col = c - ratio
        else:
            col = q * ratio + (j + way - 1) % ratio
        return remote(
            src, spot, wr_send.at[t, s, i, way], wr_recv.at[t, s, j * nrow + peer], r, col
        )

    def wr_in(t, s, seat, peer):
        spot = wr_spot(t, s, seat, peer)
        return pltpu.make_async_copy(spot, spot, wr_recv.at[t, s, seat * nrow + peer])

    def wr_keep(t, s, i):
        peer = (r + i) % nrow
        return pltpu.make_async_copy(
            wc.at[t, :, some(peer, s)], wr_spot(t, s, j, peer), local_sem.at[t, s, i]
        )

    def wr_ways(t, s, i, first, act):
        @pl.when(up)
        def _():
            act(wr_out(t, s, i, 0, first))

        @pl.when(down)
        def _():
            act(wr_out(t, s, i, 1, first))

        for k in range(1, ratio):
            act(wr_out(t, s, i, 1 + k, first))

    def start(copy):
        copy.start()

    def wait_send(copy):
        copy.wait_send()

    def seat_rows(seat):
        return pl.ds(pl.multiple_of(seat * cols_tile, cols_tile), cols_tile)

    def update_v(t):
        out_ref[...] = (out_ref if t else a_ref)[...] - half * (
            dot(vr[t], wc[t, 0], NT) + dot(vr[t], wc[t, 1], NT)
        )

    def update_w(t, seat):
        at = seat_rows(seat)
        out_ref[at] -= half * (dot(wr[t, 0, at], vt[t], NT) + dot(wr[t, 1, at], vt[t], NT))

    def turn_w(t, seat):
        at = seat_rows(seat)
        b_ref[:, at] -= half * (dot(vt[t], wr[t, 0, at], NT) + dot(vt[t], wr[t, 1, at], NT))

    for t in range(ticks):
        last = t == ticks - 1
        if t == 0:
            v_relay(0)
            v_finish(0)
        high = b_ref[...].astype(jnp.bfloat16)
        low = (b_ref[...] - high.astype(jnp.float32)).astype(jnp.bfloat16)
        part[t] = dot(high, vr[t], NN) + dot(low, vr[t], NN)
        for s in range(splits):
            for i in range(1, nrow):
                rs_out(t, s, i).start()
        for s in range(splits):
            total = part[t, some(r, s)]
            for i in range(1, nrow):
                peer = (r + i) % nrow
                rs_in(t, s, peer).wait()
                total = total + got[t, some(peer, s)]
            total = total * scaling
            head = total.astype(jnp.bfloat16)
            wc[t, 0, some(r, s)] = head
            wc[t, 1, some(r, s)] = (total - head.astype(jnp.float32)).astype(jnp.bfloat16)
            for i in range(1, nrow):
                wc_out(t, s, i).start()

            @pl.when(source)
            def _():
                wr_ways(t, s, 0, True, start)
                wr_keep(t, s, 0).start()

        if t == 0:
            @pl.when(stays)
            def _():
                vt_in.wait()

            @pl.when(jnp.logical_not(stays))
            def _():
                vt_move.wait()

        for i in range(1, nrow):
            vt_out(t, i).start()
        if t:
            update_v(t - 1)
            for seat in range(ratio):
                update_w(t - 1, seat)

        @pl.when(source)
        def _():
            for s in range(splits):
                for i in range(1, nrow):
                    wc_in(t, s, (r + i) % nrow).wait()
                    wr_ways(t, s, i, True, start)
                    wr_keep(t, s, i).start()

        @pl.when(jnp.logical_not(source))
        def _():
            for s in range(splits):
                wr_in(t, s, j, r).wait()
                wr_ways(t, s, 0, False, start)
            for s in range(splits):
                for i in range(1, nrow):
                    wr_in(t, s, j, (r + i) % nrow).wait()
                    wr_ways(t, s, i, False, start)
            for s in range(splits):
                for i in range(1, nrow):
                    wc_in(t, s, (r + i) % nrow).wait()

        if last:
            update_v(t)
        else:
            v_relay(t + 1)
            b_ref[...] -= half * (dot(wc[t, 0], vr[t], NT) + dot(wc[t, 1], vr[t], NT))
            v_finish(t + 1)

        for i in range(1, nrow):
            vt_got(t, (r + i) % nrow).wait()

        @pl.when(source)
        def _():
            for s in range(splits):
                for i in range(nrow):
                    wr_keep(t, s, i).wait()

        for k in range(ratio):
            seat = (j + k) % ratio
            if k:
                for s in range(splits):
                    for i in range(nrow):
                        wr_in(t, s, seat, (r + i) % nrow).wait()
            if last:
                update_w(t, seat)
            else:
                turn_w(t, seat)
        mine = rows(c)
        w_ref[t] = wr[t, 0, mine].astype(jnp.float32) + wr[t, 1, mine].astype(jnp.float32)

    for t in range(ticks):
        for i in range(1, links):
            v_out(t, i).wait_send()
        for i in range(links):
            for k in range(1, ratio):
                v_side(t, i, k).wait_send()
        for i in range(1, nrow):
            vt_out(t, i).wait_send()
            for s in range(splits):
                rs_out(t, s, i).wait_send()
                wc_out(t, s, i).wait_send()

        @pl.when(source)
        def _():
            for s in range(splits):
                for i in range(nrow):
                    wr_ways(t, s, i, True, wait_send)

        @pl.when(jnp.logical_not(source))
        def _():
            for s in range(splits):
                for i in range(nrow):
                    wr_ways(t, s, i, False, wait_send)


def on_device(trailing, v_panels):
    nrow = lax.axis_size("row")
    ncol = lax.axis_size("col")
    rows_tile, cols_tile = trailing.shape
    ticks, piece, depth = v_panels.shape
    ratio = rows_tile // cols_tile
    links = ncol // ratio
    splits = SPLITS if piece % (SPLITS * 16) == 0 else 1
    scaling = 1.0 / math.sqrt(rows_tile * nrow)
    dma = pltpu.SemaphoreType.DMA
    vmem = pl.BlockSpec(memory_space=pltpu.VMEM)
    return pl.pallas_call(
        functools.partial(kernel, nrow, ncol, ratio, scaling),
        out_shape=(
            jax.ShapeDtypeStruct(trailing.shape, jnp.float32),
            jax.ShapeDtypeStruct(v_panels.shape, jnp.float32),
        ),
        in_specs=[vmem, vmem],
        out_specs=(vmem, vmem),
        scratch_shapes=[
            pltpu.VMEM((cols_tile, rows_tile), jnp.float32),
            pltpu.VMEM((ticks, rows_tile, depth), jnp.bfloat16),
            pltpu.VMEM((ticks, cols_tile, depth), jnp.bfloat16),
            pltpu.VMEM((ticks, cols_tile, depth), jnp.float32),
            pltpu.VMEM((ticks, cols_tile, depth), jnp.float32),
            pltpu.VMEM((ticks, 2, cols_tile, depth), jnp.bfloat16),
            pltpu.VMEM((ticks, 2, rows_tile, depth), jnp.bfloat16),
            dma((ticks, links)),
            dma((ticks, ncol)),
            dma,
            dma,
            dma((ticks, links + nrow, ratio)),
            dma((ticks, nrow)),
            dma((ticks, splits, nrow)),
            dma((ticks, splits, nrow)),
            dma((ticks, splits, nrow)),
            dma((ticks, splits, nrow)),
            dma((ticks, splits, nrow, ratio + 1)),
            dma((ticks, splits, ncol)),
            dma((ticks, splits, nrow)),
        ],
        compiler_params=pltpu.CompilerParams(collective_id=0, has_side_effects=True),
    )(trailing, v_panels)


def solution(mesh):
    in_specs = (P("row", "col"), P(None, ("row", "col"), None))
    out_specs = (P("row", "col"), P(None, ("row", "col"), None))
    return jax.shard_map(
        on_device, mesh=mesh, in_specs=in_specs, out_specs=out_specs, check_vma=False
    )
```
